32 devices in a mesh: leaf: 2 (over y), row: 4 (over x, core), col: 4 (over z).
Axes of the slice: x: 2, y: 2, z: 4, core: 2. Of those that a mesh axis runs over, the one named last changes fastest.
Arguments:
- panel: float32 [8192, 1024], P(('leaf', 'row'), 'col'), may hold values from -1.2 to 1.2
- block_mask: int32 [64, 8], P(('leaf', 'row'), 'col'), may hold values 0 or 1
- front_rest: float32 [4096, 4096], P(('leaf', 'row'), 'col'), may hold values from -6 to 6
- row_maps: int32 [8, 4], P(('leaf', 'row')), may hold values from 0 to 3, each once within a row
- col_maps: int32 [8, 12], P(('leaf', 'col')), may hold values from 0 to 11, each once within a row
Outputs:
- parent: float32 [2048, 6144], P(('leaf', 'row'), 'col')
The draws below stay inside these ranges and needn't reach their ends.
Inputs may be any that keep to these rules, and one draw needn't show every extreme that they name: `row_maps`: each row is a permutation of 0 to 3. `col_maps`: each row is a permutation of 0 to 11; only its first 8 entries are used.
All inputs are finite; a program needn't handle non-finite values. No bound on the sum of `block_mask` on one device may be relied on, other than what follows from the above.
Results may differ from the reference program's by a relative error of at most 0.0003.
Values sent between devices are 32-bit elements; how exact they have to be, the bound alone decides.
A program may use at most 64 MiB of HBM per device.

```python
import jax
import jax.numpy as jnp
import numpy as np
from jax import lax

BLK = 128
P_SIZE = 1024
MC = 4096
PC = 6144
WR = 512
WB = 4
PCB = 12
N_LEAF = 2
N_ROW = 4
N_COL = 4


def set_ends(entries, rng, low, high):
    spot = [jax.random.randint(jax.random.fold_in(rng, axis), (), 0, length) for axis, length in enumerate(entries.shape)]
    widest = entries.shape.index(max(entries.shape))
    next_to = spot[:widest] + [(spot[widest] + 1) % entries.shape[widest]] + spot[widest + 1:]
    return entries.at[tuple(spot)].set(low).at[tuple(next_to)].set(high)


def block_scale(rng, extent, split, least, high):
    def one(axis_at, blocks):
        heights = jax.random.uniform(jax.random.fold_in(jax.random.fold_in(rng, 6), axis_at), (blocks,), jnp.float32, least / len(split), high / len(split))
        return jnp.repeat(jnp.exp(heights), extent[axis_at] // blocks).reshape((-1,) + (1,) * (len(extent) - axis_at - 1))

    factor_of = one(*split[0])
    for cut in split[1:]:
        factor_of = factor_of * one(*cut)
    return factor_of


def scatter_about(own_key, shape, deviation, bound, shards=(), held_as=jnp.bfloat16):
    loudness = block_scale(own_key, shape, shards, -0.22, 0.18) if shards else 1.0
    values = jax.random.normal(own_key, shape, jnp.float32) * deviation * loudness
    return jnp.minimum(jnp.maximum(values, -bound), bound).astype(held_as)


def setup_inputs(seed: int = 0) -> dict:
    arg_keys = jax.random.split(jax.random.key(seed), 6)
    return {
        "panel": scatter_about(arg_keys[0], (N_LEAF * MC, P_SIZE), 0.18, 1.2, ((0, 8), (1, 4)), jnp.float32),
        "block_mask": set_ends((jax.random.randint(arg_keys[1], (N_LEAF * MC // BLK, P_SIZE // BLK), 0, 4) < 3).astype(jnp.int32), jax.random.fold_in(arg_keys[1], 1), 0, 1),
        "front_rest": scatter_about(arg_keys[2], (N_LEAF * N_ROW * WR, MC), 1.0, 6.0, ((0, 8), (1, 4)), jnp.float32),
        "row_maps": jax.vmap(lambda own: jax.random.permutation(own, WB))(jax.random.split(arg_keys[3], (N_LEAF * N_ROW))).reshape((N_LEAF * N_ROW, WB)).astype(jnp.int32),
        "col_maps": jax.vmap(lambda own: jax.random.permutation(own, PCB))(jax.random.split(arg_keys[4], (N_LEAF * N_COL))).reshape((N_LEAF * N_COL, PCB)).astype(jnp.int32),
    }


def reference(panel, block_mask, front_rest, row_maps, col_maps):
    halfway = N_LEAF // 2
    win_blocks = WR // BLK
    child_blocks = MC // (BLK * N_COL)
    parent_blocks = PC // (BLK * N_COL)

    def one_child(leaf):
        leaf = leaf.astype(jnp.int32)
        rows = lax.dynamic_slice_in_dim(panel, leaf * MC, MC, 0)
        flags = lax.dynamic_slice_in_dim(block_mask, leaf * (MC // BLK), MC // BLK, 0).astype(jnp.float32)
        masked = (rows.reshape(MC // BLK, BLK, P_SIZE // BLK, BLK) * flags[:, None, :, None]).reshape(MC, P_SIZE)
        window = masked.reshape(N_ROW, MC // N_ROW, P_SIZE)[:, :WR].reshape(N_ROW * WR, P_SIZE)
        front = lax.dynamic_slice_in_dim(front_rest, leaf * (N_ROW * WR), N_ROW * WR, 0)
        update = front - jnp.dot(window, masked.T, precision=lax.Precision.HIGHEST, preferred_element_type=jnp.float32)
        rmaps = lax.dynamic_slice_in_dim(row_maps, leaf * N_ROW, N_ROW, 0)
        cmaps = lax.dynamic_slice_in_dim(col_maps, leaf * N_COL, N_COL, 0)[:, :child_blocks]
        blocks = update.reshape(N_ROW, win_blocks, BLK, N_COL, child_blocks, BLK).transpose(0, 1, 3, 4, 2, 5)
        grid_rows = jnp.arange(N_ROW, dtype=jnp.int32)[:, None, None, None]
        grid_cols = jnp.arange(N_COL, dtype=jnp.int32)[None, None, :, None]
        spread = jnp.zeros((N_ROW, win_blocks, N_COL, parent_blocks, BLK, BLK), jnp.float32)
        return spread.at[grid_rows, rmaps[:, :, None, None], grid_cols, cmaps[None, None, :, :]].set(blocks)

    spread_all = lax.map(one_child, jnp.arange(N_LEAF, dtype=jnp.int32))
    partner = np.arange(N_LEAF) ^ halfway
    summed = spread_all + spread_all[partner]
    summed = summed.reshape(N_LEAF, N_ROW, 2, win_blocks // 2, N_COL, parent_blocks, BLK, BLK)
    upper = (np.arange(N_LEAF) // halfway) % 2
    kept = summed[np.arange(N_LEAF), :, upper]
    return kept.transpose(0, 1, 2, 5, 3, 4, 6).reshape(N_LEAF * N_ROW * WR // 2, PC)
```

```python
import functools

import jax
import jax.numpy as jnp
from jax import lax
from jax.experimental import pallas as pl
from jax.experimental.pallas import tpu as pltpu
from jax.sharding import PartitionSpec as P

BLK = 128
PC = 6144
F32 = jnp.float32
BF16 = jnp.bfloat16

LEFT, RIGHT, PAIR, CROSS, DIAG = range(5)
STORE = (0, 1, 6, 7, 2, 4, 3, 5)


def split(value):
    high = value.astype(BF16)
    return high, (value - high.astype(F32)).astype(BF16)


def update_kernel(
    n_leaf, n_row, n_col,
    panel_hbm, mask_hbm, front_hbm, rows_hbm, cols_hbm,
    out_ref,
    big, panel, panel_low, front, a_cat, b_cat, snd, got, mine,
    rows_own, rows_col, rows_other, cols_own, cols_other,
    mask_s, rows_own_s, rows_col_s, rows_other_s, cols_own_s, cols_other_s,
    send, recv, sib_send, sib_recv, map_send, map_recv, loc,
):
    leaf, r, c = lax.axis_index("leaf"), lax.axis_index("row"), lax.axis_index("col")
    x, k = r // 2, r % 2
    sib = lax.rem(leaf + n_leaf // 2, n_leaf)
    upper = leaf // (n_leaf // 2) % 2
    width = panel.shape[2]
    blocks, win_blocks = front.shape[:2]
    half = win_blocks // 2
    keep = half * BLK
    lanes = width // BLK
    parents = out_ref.shape[1] // BLK
    span = 3 * width

    pair_row, x_row, diag_row = x * 2 + 1 - k, (1 - x) * 2 + k, (1 - x) * 2 + 1 - k
    is_o, is_q, is_x, is_d = r == c, pair_row == c, x_row == c, diag_row == c

    def to(row=None, column=None, other_leaf=None):
        return {
            "leaf": leaf if other_leaf is None else other_leaf,
            "row": r if row is None else row,
            "col": c if column is None else column,
        }

    def remote(src, dst, ssem, rsem, where):
        return pltpu.make_async_remote_copy(
            src_ref=src, dst_ref=dst, send_sem=ssem, recv_sem=rsem,
            device_id=where, device_id_type=pl.DeviceIdType.MESH,
        )

    def push(way, src, j, dst):
        where = {
            LEFT: lambda: to(column=c - 1), RIGHT: lambda: to(column=c + 1),
            PAIR: lambda: to(row=pair_row), CROSS: lambda: to(row=x_row), DIAG: lambda: to(row=diag_row),
        }[way]()
        return remote(big.at[src, j], big.at[dst, j], send.at[way, src, j], recv.at[dst, j], where)

    sent, gates = [], []

    def when(cond, run):
        @pl.when(cond())
        def _():
            gates.append(cond)
            run()
            gates.pop()

    def go(way, copy):
        sent.append((way, copy, tuple(gates)))
        push(way, *copy()).start()

    def settle(count):
        for way, copy, conds in sent[:count]:
            def finish():
                push(way, *copy()).wait_send()
            if conds:
                pl.when(both(*[cond() for cond in conds]))(finish)
            else:
                finish()
        del sent[:count]

    def arrive(slot, j):
        push(PAIR, slot, j, slot).wait_recv()

    def both(*conds):
        total = conds[0]
        for cond in conds[1:]:
            total = jnp.logical_and(total, cond)
        return total

    def fetch(src, dst, n):
        return pltpu.make_async_copy(src, dst, loc.at[n])

    get_rows = fetch(rows_hbm, rows_own, 0)
    get_mask = fetch(mask_hbm, mask_s, 1)
    get_win = fetch(panel_hbm.at[pl.ds(0, win_blocks)], panel, 2)
    rest = pl.ds(win_blocks, blocks - win_blocks)
    get_low = fetch(panel_hbm.at[rest], panel_low, 3)
    get_cols = fetch(cols_hbm, cols_own, 4)
    get_front = [
        fetch(front_hbm.at[:, :, pl.ds(m * BLK, BLK)], front.at[m], 5 + m) for m in range(blocks)
    ]
    get_rows.start()
    get_mask.start()
    get_win.start()
    get_low.start()
    get_cols.start()
    for copy in get_front:
        copy.start()

    barrier = pltpu.get_barrier_semaphore()

    def greet(where):
        pl.semaphore_signal(barrier, inc=1, device_id=where, device_id_type=pl.DeviceIdType.MESH)

    has_left, has_right = c >= 1, c + 1 < n_col

    @pl.when(has_left)
    def _():
        greet(to(column=c - 1))

    @pl.when(has_right)
    def _():
        greet(to(column=c + 1))

    greet(to(row=x_row))
    greet(to(row=diag_row))
    greet(to(other_leaf=sib))
    greet(to(row=pair_row))

    first_kept, first_sent = upper * half, (1 - upper) * half
    order_own = [first_sent + i for i in range(half)] + [first_kept + i for i in range(half)]
    order_other = [first_kept + i for i in range(half)] + [first_sent + i for i in range(half)]

    def place(rows_s, parent):
        at = jnp.int32(0)
        for m in range(1, win_blocks):
            at = jnp.where(rows_s[0, m] == parent, jnp.int32(m), at)
        return at

    def pick(values, at):
        total = jnp.int32(0)
        for m, value in enumerate(values):
            total = total + jnp.where(at == m, value, jnp.int32(0))
        return total

    get_rows.wait()
    own_rows = fetch(rows_own, rows_own_s, 0)
    own_rows.start()
    get_mask.wait()
    own_rows.wait()
    natural = [place(rows_own_s, parent) for parent in order_own]

    def window_base(column):
        return jnp.where(r == column, 0, blocks)

    win_at = window_base(c)
    low_at = jnp.where(is_o, win_blocks, 2 * blocks)

    get_win.wait()
    for b in range(win_blocks):
        block = panel[natural[b]]
        for h in range(lanes):
            cut = slice(h * BLK, (h + 1) * BLK)
            flag = pick([mask_s[h, m] for m in range(win_blocks)], natural[b]).astype(F32)
            big[win_at + b, c, :, cut] = block[:, cut] * flag
    get_low.wait()
    for b in range(win_blocks):
        at = win_blocks + b
        for h in range(lanes):
            cut = slice(h * BLK, (h + 1) * BLK)
            big[low_at + b, c, :, cut] = panel_low[b, :, cut] * mask_s[h, at].astype(F32)

    pl.semaphore_wait(barrier, 4 + has_left.astype(jnp.int32) + has_right.astype(jnp.int32))

    transit = blocks + win_blocks

    def goal(s):
        return pair_row if s < 2 else (1 - x) * 2 + (s - 2)

    def low_slot(s, column):
        block = s if s < 2 else 2 + k
        return jnp.where(goal(s) == column, win_blocks + block, transit + s)

    def has(side):
        return has_right if side else has_left

    def next_of(side):
        return c + 1 if side else c - 1

    def from_at(side, d):
        return c - d if side else c + d

    def there(side, d):
        return from_at(side, d) >= 0 if side else from_at(side, d) < n_col

    def window_on(b, d, side):
        when(lambda: has(side), lambda: go(
            RIGHT if side else LEFT,
            lambda: (win_at + b, from_at(side, d), window_base(next_of(side)) + b),
        ))

    def hand_out(slot, j):
        for way in (CROSS, PAIR):
            go(way, lambda: (slot(), j(), slot()))

    def take_window(b, d):
        for side in (0, 1):
            def run(side=side):
                arrive(win_at + b, from_at(side, d))
                window_on(b, d, side)
                when(lambda: is_o, lambda: hand_out(lambda: b, lambda: from_at(side, d)))
            when(lambda side=side: there(side, d), run)

    def ahead(s, side):
        return goal(s) > c if side else goal(s) < c

    def low_on(s, d, side):
        go(RIGHT if side else LEFT, lambda: (low_slot(s, c), from_at(side, d), low_slot(s, next_of(side))))

    def take_low(s, d):
        for side in (0, 1):
            def wanted(side=side):
                return both(there(side, d), jnp.logical_or(ahead(s, side), goal(s) == c))

            def run(side=side):
                arrive(low_slot(s, c), from_at(side, d))
                when(lambda: ahead(s, side), lambda: low_on(s, d, side))
                when(lambda: goal(s) == c, lambda: hand_out(lambda: low_slot(s, c), lambda: from_at(side, d)))
            when(wanted, run)

    def own_low(side):
        for s in LOW:
            def run(s=s):
                arrive(transit + s, c)
                low_on(s, 0, side)
            when(lambda s=s: ahead(s, side), run)

    LOW = (2, 3, 0, 1)

    def not_o():
        return jnp.logical_not(is_o)

    def owner():
        return is_o

    def inner():
        return both(has_left, has_right)

    def outer():
        return jnp.logical_not(inner())

    def scatter():
        go(CROSS, lambda: (low_at + 2 + k, c, transit + 2 + k))
        go(DIAG, lambda: (low_at + 3 - k, c, transit + 2 + k))
        for s in range(2):
            go(PAIR, lambda s=s: (low_at + s, c, transit + s))

    def spread(slots):
        for slot in slots:
            hand_out(lambda slot=slot: slot, lambda: c)

    def at_source(side):
        return c == 0 if side else c == n_col - 1

    def own_late(side):
        for b in range(half, win_blocks):
            window_on(b, 0, side)

    def map_copy(src, dst, n, where, arrived=None):
        return remote(src, dst, map_send.at[n], map_recv.at[n if arrived is None else arrived], where)

    get_cols.wait()
    to_sib_cols = map_copy(cols_own, cols_other, 0, to(other_leaf=sib))
    to_sib_cols.start()
    rows_cross = map_copy(rows_own, rows_col, 1, to(row=x_row))
    rows_pair = map_copy(rows_own, rows_col, 2, to(row=pair_row), 1)
    rows_pass = map_copy(rows_col, rows_col, 2, to(row=pair_row), 1)
    rows_stay = fetch(rows_own, rows_col, 0)
    to_sib_rows = map_copy(rows_col, rows_other, 3, to(other_leaf=sib))

    def rows_from_owner():
        rows_cross.start()
        rows_pair.start()
        rows_stay.start()

    when(owner, rows_from_owner)

    def by_cross(slot, j):
        if slot < win_blocks:
            other = is_x
        elif slot < win_blocks + 2:
            other = is_d
        else:
            other = both(k == slot - win_blocks - 2, jnp.logical_or(is_o, is_q))
        return jnp.where(c == j, is_x, other)

    def by_pair(slot, j):
        if slot < win_blocks:
            other = jnp.logical_or(is_q, is_d)
        elif slot < win_blocks + 2:
            other = jnp.logical_or(is_o, is_x)
        else:
            other = k != slot - win_blocks - 2
        return jnp.where(c == j, jnp.logical_or(is_q, is_d), other)

    def collect(slots):
        for slot in slots:
            for j in range(n_col):
                def run(slot=slot, j=j):
                    arrive(slot, j)
                    go(PAIR, lambda: (slot, j, slot))
                when(lambda slot=slot, j=j: by_cross(slot, j), run)
        for slot in slots:
            for j in range(n_col):
                when(lambda slot=slot, j=j: by_pair(slot, j), lambda: arrive(slot, j))

    def lay_rows(b):
        rows = slice(b * BLK, (b + 1) * BLK)
        for j in range(n_col):
            high, low = split(big[win_at + b, j])
            at = j * span
            a_cat[rows, at:at + width] = high
            a_cat[rows, at + width:at + 2 * width] = high
            a_cat[rows, at + 2 * width:at + span] = low

    def lay_columns(slot):
        rows = slice(STORE.index(slot) * BLK, (STORE.index(slot) + 1) * BLK)
        for j in range(n_col):
            high, low = split(big[slot, j])
            at = j * span
            b_cat[rows, at:at + width] = high
            b_cat[rows, at + width:at + 2 * width] = low
            b_cat[rows, at + 2 * width:at + span] = high

    def multiply(group, part):
        product = lax.dot_general(
            a_cat[part * keep:(part + 1) * keep, :], b_cat[group * 2 * BLK:(group + 1) * 2 * BLK, :],
            (((1,), (1,)), ((), ())), preferred_element_type=F32,
        )
        into = mine if part else snd
        for i in range(2):
            slot = STORE[group * 2 + i]
            column = natural_col[slot] if slot < win_blocks else slot
            for b in range(half):
                into[slot, b * BLK:(b + 1) * BLK, :] = (
                    front[column, natural[part * half + b]] - product[b * BLK:(b + 1) * BLK, i * BLK:(i + 1) * BLK]
                )

    def sibling(slot):
        return remote(snd.at[slot], got.at[slot], sib_send.at[slot], sib_recv.at[slot], to(other_leaf=sib))

    def group_out(group):
        slots = STORE[group * 2:group * 2 + 2]
        for slot in slots:
            lay_columns(slot)
        multiply(group, 0)
        for slot in slots:
            sibling(slot).start()

    def late(b):
        for d in range(1, n_col):
            take_window(b, d)

    def maps_in():
        when(owner, lambda: rows_stay.wait())
        when(not_o, lambda: rows_cross.wait_recv())
        when(lambda: is_x, lambda: rows_pass.start())
        to_sib_rows.start()
        to_col_s = fetch(rows_col, rows_col_s, 0)
        to_col_s.start()
        to_col_s.wait()

    def first_out():
        collect(STORE[:2])
        for b in range(half):
            lay_rows(b)
        for copy in get_front:
            copy.wait()
        group_out(0)

    def middle_inner():
        for d in range(1, n_col):
            for s in LOW:
                take_low(s, d)
        for side in (0, 1):
            when(lambda side=side: jnp.logical_not(at_source(side)), functools.partial(own_late, side))
        first_out()
        late(half)
        collect(STORE[2:4])
        group_out(1)
        collect(STORE[4:6])
        group_out(2)
        late(half + 1)
        collect(STORE[6:])
        group_out(3)

    def middle_outer():
        first_out()
        for s in LOW[:3]:
            for d in range(1, n_col):
                take_low(s, d)
        for side in (0, 1):
            when(lambda side=side: jnp.logical_not(at_source(side)), functools.partial(own_late, side))
        when(owner, functools.partial(late, half))
        collect(STORE[2:4])
        group_out(1)
        for d in range(1, n_col):
            take_low(LOW[3], d)
        collect(STORE[4:6])
        group_out(2)
        when(owner, functools.partial(late, half + 1))
        collect(STORE[6:])
        group_out(3)
        for b in range(half, win_blocks):
            when(not_o, functools.partial(late, b))

    for b in range(half):
        for side in (0, 1):
            window_on(b, 0, side)
    when(not_o, scatter)
    for side in (0, 1):
        def source(side=side):
            own_low(side)
            own_late(side)
        when(lambda side=side: at_source(side), source)

    SPREAD = (range(half), range(win_blocks, blocks), range(half, win_blocks))
    for d in range(1, n_col):
        for b in range(half):
            take_window(b, d)
        when(owner, functools.partial(spread, SPREAD[d - 1]))
        for side in (0, 1):
            last = 0 if side else n_col - 1
            when(lambda side=side, d=d, last=last: from_at(side, d) == last, functools.partial(own_low, side))

    maps_in()
    natural_col = [place(rows_col_s, parent) for parent in order_own]
    when(inner, middle_inner)
    when(outer, middle_outer)
    for b in range(half, win_blocks):
        lay_rows(b)
    for group in range(blocks // 2):
        multiply(group, 1)
    settle(len(sent))

    to_sib_cols.wait_recv()
    to_sib_rows.wait_recv()
    to_own = fetch(cols_own, cols_own_s, 1)
    to_other = fetch(cols_other, cols_other_s, 2)
    to_rows = fetch(rows_other, rows_other_s, 3)
    to_own.start()
    to_other.start()
    to_rows.start()
    to_own.wait()
    to_other.wait()
    to_rows.wait()
    natural_other = [place(rows_other_s, parent) for parent in order_other]

    def spots(cols_s, naturals):
        values = [cols_s[0, m] for m in range(blocks)]
        return [pick(values[:win_blocks], naturals[o]) if o < win_blocks else values[o] for o in range(blocks)]

    spot_own, spot_other = spots(cols_own_s, natural_col), spots(cols_other_s, natural_other)

    for o in range(blocks):
        sibling(o).wait_recv()
    for t in range(parents):
        total = None
        for spot, held in ((spot_own, mine), (spot_other, got)):
            at, found = jnp.int32(0), jnp.int32(0)
            for o in range(blocks):
                hit = spot[o] == t
                at, found = jnp.where(hit, jnp.int32(o), at), jnp.where(hit, jnp.int32(1), found)
            term = held[at] * found.astype(F32)
            total = term if total is None else total + term
        out_ref[:, t * BLK:(t + 1) * BLK] = total

    for o in range(blocks):
        sibling(o).wait_send()
    to_sib_cols.wait_send()
    to_sib_rows.wait_send()
    when(owner, lambda: rows_cross.wait_send())
    when(owner, lambda: rows_pair.wait_send())
    when(lambda: is_x, lambda: rows_pass.wait_send())


def body(sizes, panel, block_mask, front_rest, row_maps, col_maps):
    n_leaf, n_row, n_col = sizes
    local_rows, width = panel.shape
    win_rows, front_cols = front_rest.shape
    keep = win_rows // 2
    blocks = front_cols // BLK
    win_blocks = win_rows // BLK
    parent_cols = PC // n_col
    any_space = pl.BlockSpec(memory_space=pl.ANY)
    dma = pltpu.SemaphoreType.DMA
    slots = 2 * blocks + win_blocks
    rows_type, cols_type = row_maps.dtype, col_maps.dtype
    return pl.pallas_call(
        functools.partial(update_kernel, n_leaf, n_row, n_col),
        out_shape=jax.ShapeDtypeStruct((keep, parent_cols), F32),
        in_specs=[any_space] * 5,
        out_specs=pl.BlockSpec(memory_space=pltpu.VMEM),
        scratch_shapes=[
            pltpu.VMEM((slots, n_col, BLK, width), F32),
            pltpu.VMEM((win_blocks, BLK, width), F32),
            pltpu.VMEM((blocks - win_blocks, BLK, width), F32),
            pltpu.VMEM((blocks, win_blocks, BLK, BLK), F32),
            pltpu.VMEM((win_rows, 3 * n_col * width), BF16),
            pltpu.VMEM((blocks * BLK, 3 * n_col * width), BF16),
            pltpu.VMEM((blocks, keep, BLK), F32),
            pltpu.VMEM((blocks, keep, BLK), F32),
            pltpu.VMEM((blocks, keep, BLK), F32),
            pltpu.VMEM(row_maps.shape, rows_type), pltpu.VMEM(row_maps.shape, rows_type),
            pltpu.VMEM(row_maps.shape, rows_type),
            pltpu.VMEM(col_maps.shape, cols_type), pltpu.VMEM(col_maps.shape, cols_type),
            pltpu.SMEM(block_mask.shape[::-1], block_mask.dtype),
            pltpu.SMEM(row_maps.shape, rows_type), pltpu.SMEM(row_maps.shape, rows_type),
            pltpu.SMEM(row_maps.shape, rows_type),
            pltpu.SMEM(col_maps.shape, cols_type), pltpu.SMEM(col_maps.shape, cols_type),
            dma((5, slots, n_col)), dma((slots, n_col)),
            dma((blocks,)), dma((blocks,)), dma((4,)), dma((4,)), dma((5 + blocks,)),
        ],
        compiler_params=pltpu.CompilerParams(
            collective_id=0, has_side_effects=True, vmem_limit_bytes=60 * 1024 * 1024
        ),
        name="update",
    )(
        panel.reshape(local_rows // BLK, BLK, width), block_mask.T,
        front_rest.reshape(win_blocks, BLK, front_cols), row_maps, col_maps,
    )


def solution(mesh):
    sizes = mesh.shape["leaf"], mesh.shape["row"], mesh.shape["col"]
    return jax.shard_map(
        functools.partial(body, sizes),
        mesh=mesh,
        in_specs=(
            P(("leaf", "row"), "col"),
            P(("leaf", "row"), "col"),
            P(("leaf", "row"), "col"),
            P(("leaf", "row"), None),
            P(("leaf", "col"), None),
        ),
        out_specs=P(("leaf", "row"), "col"),
        check_vma=False,
    )
```

```python
import functools

import jax
import jax.numpy as jnp
from jax import lax
from jax.experimental import pallas as pl
from jax.experimental.pallas import tpu as pltpu
from jax.sharding import PartitionSpec as P

BLK = 128
PC = 6144
F32 = jnp.float32
BF16 = jnp.bfloat16

LEFT, RIGHT, PAIR, CROSS, DIAG = range(5)
GROUPS = ((0, 1), (6, 7), (2, 4), (3,), (5,))
STORE = tuple(slot for group in GROUPS for slot in group)
INNER = (
    "S7", "S1", "A1", "S0", "A2", "S2", "S6", "S3", "S4", "S5", "x01", "x21",
    "x31", "M", "x02", "x11", "x22", "x32", "x12", "L", "G0", "w21", "G1", "w22",
    "w31", "w32o", "G4", "G2", "G3", "w32n",
)
OUTER = (
    "S3", "S2", "x21", "x31", "M", "x22", "S6", "S0", "S7", "A2", "A1", "x23",
    "A3", "S1", "x03", "x32", "x02", "G0", "S5", "S4", "L", "w21o", "x01", "x33",
    "x11", "G1", "w22o", "w23o", "w22n", "w31o", "x13", "x12", "G2", "G4", "w31n", "w32o",
    "w32n", "w33o", "w21n", "G3", "w33n", "w23n",
)


def split(value):
    high = value.astype(BF16)
    return high, (value - high.astype(F32)).astype(BF16)


def update_kernel(
    n_leaf, n_row, n_col,
    panel_hbm, mask_hbm, front_hbm, rows_hbm, cols_hbm,
    out_ref,
    big, panel, panel_low, front, a_cat, b_cat, snd, got, mine,
    rows_own, rows_col, rows_other, cols_own, cols_other,
    mask_s, rows_own_s, rows_col_s, rows_other_s, cols_own_s, cols_other_s,
    send, recv, sib_send, sib_recv, map_send, map_recv, loc,
):
    leaf, r, c = lax.axis_index("leaf"), lax.axis_index("row"), lax.axis_index("col")
    x, k = r // 2, r % 2
    sib = lax.rem(leaf + n_leaf // 2, n_leaf)
    upper = leaf // (n_leaf // 2) % 2
    width = panel.shape[2]
    blocks, win_blocks = front.shape[:2]
    half = win_blocks // 2
    keep = half * BLK
    lanes = width // BLK
    parents = out_ref.shape[1] // BLK
    span = 3 * width

    pair_row, x_row, diag_row = x * 2 + 1 - k, (1 - x) * 2 + k, (1 - x) * 2 + 1 - k
    is_o, is_q, is_x, is_d = r == c, pair_row == c, x_row == c, diag_row == c

    def to(row=None, column=None, other_leaf=None):
        return {
            "leaf": leaf if other_leaf is None else other_leaf,
            "row": r if row is None else row,
            "col": c if column is None else column,
        }

    def remote(src, dst, ssem, rsem, where):
        return pltpu.make_async_remote_copy(
            src_ref=src, dst_ref=dst, send_sem=ssem, recv_sem=rsem,
            device_id=where, device_id_type=pl.DeviceIdType.MESH,
        )

    def push(way, src, j, dst):
        where = {
            LEFT: lambda: to(column=c - 1), RIGHT: lambda: to(column=c + 1),
            PAIR: lambda: to(row=pair_row), CROSS: lambda: to(row=x_row), DIAG: lambda: to(row=diag_row),
        }[way]()
        return remote(big.at[src, j], big.at[dst, j], send.at[way, src, j], recv.at[dst, j], where)

    sent, gates = [], []

    def when(cond, run):
        @pl.when(cond())
        def _():
            gates.append(cond)
            run()
            gates.pop()

    def go(way, copy):
        sent.append((way, copy, tuple(gates)))
        push(way, *copy()).start()

    def settle(copies, depth):
        for way, copy, conds in copies:
            def finish():
                push(way, *copy()).wait_send()
            if conds[depth:]:
                pl.when(both(*[cond() for cond in conds[depth:]]))(finish)
            else:
                finish()

    def arrive(slot, j):
        push(PAIR, slot, j, slot).wait_recv()

    def both(*conds):
        total = conds[0]
        for cond in conds[1:]:
            total = jnp.logical_and(total, cond)
        return total

    def fetch(src, dst, n):
        return pltpu.make_async_copy(src, dst, loc.at[n])

    get_rows = fetch(rows_hbm, rows_own, 0)
    get_rows_s = fetch(rows_hbm, rows_own_s, 5 + blocks)
    get_mask = fetch(mask_hbm, mask_s, 1)
    get_win = fetch(panel_hbm.at[pl.ds(0, win_blocks)], panel, 2)
    rest = pl.ds(win_blocks, blocks - win_blocks)
    get_low = fetch(panel_hbm.at[rest], panel_low, 3)
    get_cols = fetch(cols_hbm, cols_own, 4)
    get_front = [
        fetch(front_hbm.at[:, :, pl.ds(m * BLK, BLK)], front.at[m], 5 + m) for m in range(blocks)
    ]
    get_rows_s.start()
    get_mask.start()
    get_win.start()
    get_low.start()
    get_rows.start()
    get_cols.start()
    for copy in get_front:
        copy.start()

    barrier = pltpu.get_barrier_semaphore()

    def greet(where):
        pl.semaphore_signal(barrier, inc=1, device_id=where, device_id_type=pl.DeviceIdType.MESH)

    has_left, has_right = c >= 1, c + 1 < n_col

    @pl.when(has_left)
    def _():
        greet(to(column=c - 1))

    @pl.when(has_right)
    def _():
        greet(to(column=c + 1))

    greet(to(row=x_row))
    greet(to(row=diag_row))
    greet(to(other_leaf=sib))
    greet(to(row=pair_row))

    first_kept, first_sent = upper * half, (1 - upper) * half
    order_own = [first_sent + i for i in range(half)] + [first_kept + i for i in range(half)]
    order_other = [first_kept + i for i in range(half)] + [first_sent + i for i in range(half)]

    def place(rows_s, parent):
        at = jnp.int32(0)
        for m in range(1, win_blocks):
            at = jnp.where(rows_s[0, m] == parent, jnp.int32(m), at)
        return at

    def pick(values, at):
        total = jnp.int32(0)
        for m, value in enumerate(values):
            total = total + jnp.where(at == m, value, jnp.int32(0))
        return total

    get_mask.wait()
    get_rows_s.wait()
    natural = [place(rows_own_s, parent) for parent in order_own]

    def window_base(column):
        return jnp.where(r == column, 0, blocks)

    win_at = window_base(c)
    low_at = jnp.where(is_o, win_blocks, 2 * blocks)

    get_win.wait()
    for b in range(win_blocks):
        block = panel[natural[b]]
        for h in range(lanes):
            cut = slice(h * BLK, (h + 1) * BLK)
            flag = pick([mask_s[h, m] for m in range(win_blocks)], natural[b]).astype(F32)
            big[win_at + b, c, :, cut] = block[:, cut] * flag
    get_low.wait()
    for b in range(win_blocks):
        at = win_blocks + b
        for h in range(lanes):
            cut = slice(h * BLK, (h + 1) * BLK)
            big[low_at + b, c, :, cut] = panel_low[b, :, cut] * mask_s[h, at].astype(F32)

    pl.semaphore_wait(barrier, 4 + has_left.astype(jnp.int32) + has_right.astype(jnp.int32))

    transit = blocks + win_blocks

    def goal(s):
        return pair_row if s < 2 else (1 - x) * 2 + (s - 2)

    def low_slot(s, column):
        block = s if s < 2 else 2 + k
        return jnp.where(goal(s) == column, win_blocks + block, transit + s)

    def has(side):
        return has_right if side else has_left

    def next_of(side):
        return c + 1 if side else c - 1

    def from_at(side, d):
        return c - d if side else c + d

    def there(side, d):
        return from_at(side, d) >= 0 if side else from_at(side, d) < n_col

    def window_on(b, d, side):
        when(lambda: has(side), lambda: go(
            RIGHT if side else LEFT,
            lambda: (win_at + b, from_at(side, d), window_base(next_of(side)) + b),
        ))

    def hand_out(slot, j):
        for way in (CROSS, PAIR):
            go(way, lambda: (slot(), j(), slot()))

    def take_window(b, d):
        for side in (0, 1):
            def run(side=side):
                arrive(win_at + b, from_at(side, d))
                window_on(b, d, side)
                when(lambda: is_o, lambda: hand_out(lambda: b, lambda: from_at(side, d)))
            when(lambda side=side: there(side, d), run)

    def ahead(s, side):
        return goal(s) > c if side else goal(s) < c

    def low_on(s, d, side):
        go(RIGHT if side else LEFT, lambda: (low_slot(s, c), from_at(side, d), low_slot(s, next_of(side))))

    def take_low(s, d):
        for side in (0, 1):
            def wanted(side=side):
                return both(there(side, d), jnp.logical_or(ahead(s, side), goal(s) == c))

            def run(side=side):
                arrive(low_slot(s, c), from_at(side, d))
                when(lambda: ahead(s, side), lambda: low_on(s, d, side))
                when(lambda: goal(s) == c, lambda: hand_out(lambda: low_slot(s, c), lambda: from_at(side, d)))
            when(wanted, run)

    def own_low(side):
        for s in LOW:
            def run(s=s):
                arrive(transit + s, c)
                low_on(s, 0, side)
            when(lambda s=s: ahead(s, side), run)

    LOW = (2, 3, 0, 1)

    def not_o():
        return jnp.logical_not(is_o)

    def owner():
        return is_o

    def inner():
        return both(has_left, has_right)

    def outer():
        return jnp.logical_not(inner())

    def near():
        return jnp.logical_or(is_o, is_q)

    def far():
        return jnp.logical_not(near())

    def scatter():
        go(CROSS, lambda: (low_at + 2 + k, c, transit + 2 + k))
        go(DIAG, lambda: (low_at + 3 - k, c, transit + 2 + k))
        for s in range(2):
            go(PAIR, lambda s=s: (low_at + s, c, transit + s))

    def spread(slots):
        for slot in slots:
            hand_out(lambda slot=slot: slot, lambda: c)

    def at_source(side):
        return c == 0 if side else c == n_col - 1

    def own_late(side):
        for b in range(half, win_blocks):
            window_on(b, 0, side)

    def map_copy(src, dst, n, where, arrived=None):
        return remote(src, dst, map_send.at[n], map_recv.at[n if arrived is None else arrived], where)

    get_rows.wait()
    get_cols.wait()
    to_sib_cols = map_copy(cols_own, cols_other, 0, to(other_leaf=sib))
    to_sib_cols.start()
    rows_cross = map_copy(rows_own, rows_col, 1, to(row=x_row))
    rows_pair = map_copy(rows_own, rows_col, 2, to(row=pair_row), 1)
    rows_pass = map_copy(rows_col, rows_col, 2, to(row=pair_row), 1)
    rows_stay = fetch(rows_own, rows_col, 0)
    to_sib_rows = map_copy(rows_col, rows_other, 3, to(other_leaf=sib))

    def rows_from_owner():
        rows_cross.start()
        rows_pair.start()
        rows_stay.start()

    when(owner, rows_from_owner)

    def by_cross(slot, j):
        if slot < win_blocks:
            other = is_x
        elif slot < win_blocks + 2:
            other = is_d
        else:
            other = both(k == slot - win_blocks - 2, jnp.logical_or(is_o, is_q))
        return jnp.where(c == j, is_x, other)

    def by_pair(slot, j):
        if slot < win_blocks:
            other = jnp.logical_or(is_q, is_d)
        elif slot < win_blocks + 2:
            other = jnp.logical_or(is_o, is_x)
        else:
            other = k != slot - win_blocks - 2
        return jnp.where(c == j, jnp.logical_or(is_q, is_d), other)

    def collect(slots):
        for slot in slots:
            for j in range(n_col):
                def run(slot=slot, j=j):
                    arrive(slot, j)
                    go(PAIR, lambda: (slot, j, slot))
                when(lambda slot=slot, j=j: by_cross(slot, j), run)
        for slot in slots:
            for j in range(n_col):
                when(lambda slot=slot, j=j: by_pair(slot, j), lambda: arrive(slot, j))

    def lay_rows(b):
        rows = slice(b * BLK, (b + 1) * BLK)
        for j in range(n_col):
            high, low = split(big[win_at + b, j])
            at = j * span
            a_cat[rows, at:at + width] = high
            a_cat[rows, at + width:at + 2 * width] = high
            a_cat[rows, at + 2 * width:at + span] = low

    def lay_columns(slot):
        rows = slice(STORE.index(slot) * BLK, (STORE.index(slot) + 1) * BLK)
        for j in range(n_col):
            high, low = split(big[slot, j])
            at = j * span
            b_cat[rows, at:at + width] = high
            b_cat[rows, at + width:at + 2 * width] = low
            b_cat[rows, at + 2 * width:at + span] = high

    def multiply(slots, part):
        first = STORE.index(slots[0])
        product = lax.dot_general(
            a_cat[part * keep:(part + 1) * keep, :], b_cat[first * BLK:(first + len(slots)) * BLK, :],
            (((1,), (1,)), ((), ())), preferred_element_type=F32,
        )
        into = mine if part else snd
        for i, slot in enumerate(slots):
            column = place(rows_col_s, order_own[slot]) if slot < win_blocks else slot
            for b in range(half):
                into[slot, b * BLK:(b + 1) * BLK, :] = (
                    front[column, natural[part * half + b]] - product[b * BLK:(b + 1) * BLK, i * BLK:(i + 1) * BLK]
                )

    def sibling(slot):
        return remote(snd.at[slot], got.at[slot], sib_send.at[slot], sib_recv.at[slot], to(other_leaf=sib))

    def group_out(group):
        slots = GROUPS[group]
        collect(slots)
        if group == 0:
            for b in range(half):
                lay_rows(b)
            for copy in get_front:
                copy.wait()
        for slot in slots:
            lay_columns(slot)
        multiply(slots, 0)
        for slot in slots:
            sibling(slot).start()

    def maps_in():
        when(owner, lambda: rows_stay.wait())
        when(not_o, lambda: rows_cross.wait_recv())
        when(lambda: is_x, lambda: rows_pass.start())
        to_sib_rows.start()
        to_col_s = fetch(rows_col, rows_col_s, 0)
        to_col_s.start()
        to_col_s.wait()

    def windows(d):
        for b in range(half):
            take_window(b, d)
        for side in (0, 1):
            last = 0 if side else n_col - 1
            when(lambda side=side, last=last: from_at(side, d) == last, functools.partial(own_low, side))

    def own_rest():
        for side in (0, 1):
            when(lambda side=side: jnp.logical_not(at_source(side)), functools.partial(own_late, side))

    def step(token):
        kind, rest = token[0], token[1:]
        if kind == "A":
            windows(int(rest))
        elif kind == "S":
            when(owner, functools.partial(spread, (int(rest),)))
        elif kind == "M":
            maps_in()
        elif kind == "L":
            own_rest()
        elif kind == "G":
            group_out(int(rest))
        elif kind == "x":
            take_low(int(rest[0]), int(rest[1]))
        else:
            run = functools.partial(take_window, int(rest[0]), int(rest[1]))
            if rest[2:]:
                when(owner if rest[2:] == "o" else not_o, run)
            else:
                run()

    def follow(tokens):
        for token in tokens:
            step(token)

    for b in range(half):
        for side in (0, 1):
            window_on(b, 0, side)
    when(not_o, scatter)
    for side in (0, 1):
        def source(side=side):
            own_low(side)
            own_late(side)
        when(lambda side=side: at_source(side), source)

    first = len(sent)
    parts = []
    for mine_too, tokens in ((inner, INNER), (outer, OUTER)):
        before = len(sent)
        when(mine_too, functools.partial(follow, tokens))
        parts.append((mine_too, sent[before:]))
    for b in range(half, win_blocks):
        lay_rows(b)
    for slots in GROUPS:
        multiply(slots, 1)
    for mine_too, copies in parts:
        when(mine_too, functools.partial(settle, copies, 1))
    settle(sent[:first], 0)

    to_sib_cols.wait_recv()
    to_sib_rows.wait_recv()
    to_own = fetch(cols_own, cols_own_s, 1)
    to_other = fetch(cols_other, cols_other_s, 2)
    to_rows = fetch(rows_other, rows_other_s, 3)
    to_own.start()
    to_other.start()
    to_rows.start()
    to_own.wait()
    to_other.wait()
    to_rows.wait()
    natural_col = [place(rows_col_s, parent) for parent in order_own]
    natural_other = [place(rows_other_s, parent) for parent in order_other]

    def spots(cols_s, naturals):
        values = [cols_s[0, m] for m in range(blocks)]
        return [pick(values[:win_blocks], naturals[o]) if o < win_blocks else values[o] for o in range(blocks)]

    spot_own, spot_other = spots(cols_own_s, natural_col), spots(cols_other_s, natural_other)

    def source_of(spot, t):
        at, found = jnp.int32(0), jnp.int32(0)
        for o in range(blocks):
            hit = spot[o] == t
            at, found = jnp.where(hit, jnp.int32(o), at), jnp.where(hit, jnp.int32(1), found)
        return at, found.astype(F32)

    sources = [(source_of(spot_own, t), source_of(spot_other, t)) for t in range(parents)]
    for o in range(blocks):
        sibling(o).wait_recv()
    for t, ((at, found), (at_got, found_got)) in enumerate(sources):
        out_ref[:, t * BLK:(t + 1) * BLK] = mine[at] * found + got[at_got] * found_got

    for o in range(blocks):
        sibling(o).wait_send()
    to_sib_cols.wait_send()
    to_sib_rows.wait_send()
    when(owner, lambda: rows_cross.wait_send())
    when(owner, lambda: rows_pair.wait_send())
    when(lambda: is_x, lambda: rows_pass.wait_send())


def body(sizes, panel, block_mask, front_rest, row_maps, col_maps):
    n_leaf, n_row, n_col = sizes
    local_rows, width = panel.shape
    win_rows, front_cols = front_rest.shape
    keep = win_rows // 2
    blocks = front_cols // BLK
    win_blocks = win_rows // BLK
    parent_cols = PC // n_col
    any_space = pl.BlockSpec(memory_space=pl.ANY)
    dma = pltpu.SemaphoreType.DMA
    slots = 2 * blocks + win_blocks
    rows_type, cols_type = row_maps.dtype, col_maps.dtype
    return pl.pallas_call(
        functools.partial(update_kernel, n_leaf, n_row, n_col),
        out_shape=jax.ShapeDtypeStruct((keep, parent_cols), F32),
        in_specs=[any_space] * 5,
        out_specs=pl.BlockSpec(memory_space=pltpu.VMEM),
        scratch_shapes=[
            pltpu.VMEM((slots, n_col, BLK, width), F32),
            pltpu.VMEM((win_blocks, BLK, width), F32),
            pltpu.VMEM((blocks - win_blocks, BLK, width), F32),
            pltpu.VMEM((blocks, win_blocks, BLK, BLK), F32),
            pltpu.VMEM((win_rows, 3 * n_col * width), BF16),
            pltpu.VMEM((blocks * BLK, 3 * n_col * width), BF16),
            pltpu.VMEM((blocks, keep, BLK), F32),
            pltpu.VMEM((blocks, keep, BLK), F32),
            pltpu.VMEM((blocks, keep, BLK), F32),
            pltpu.VMEM(row_maps.shape, rows_type), pltpu.VMEM(row_maps.shape, rows_type),
            pltpu.VMEM(row_maps.shape, rows_type),
            pltpu.VMEM(col_maps.shape, cols_type), pltpu.VMEM(col_maps.shape, cols_type),
            pltpu.SMEM(block_mask.shape[::-1], block_mask.dtype),
            pltpu.SMEM(row_maps.shape, rows_type), pltpu.SMEM(row_maps.shape, rows_type),
            pltpu.SMEM(row_maps.shape, rows_type),
            pltpu.SMEM(col_maps.shape, cols_type), pltpu.SMEM(col_maps.shape, cols_type),
            dma((5, slots, n_col)), dma((slots, n_col)),
            dma((blocks,)), dma((blocks,)), dma((4,)), dma((4,)), dma((6 + blocks,)),
        ],
        compiler_params=pltpu.CompilerParams(
            collective_id=0, has_side_effects=True, vmem_limit_bytes=40 * 1024 * 1024
        ),
        name="update",
    )(*[pltpu.with_memory_space_constraint(value, pltpu.HBM) for value in (
        panel.reshape(local_rows // BLK, BLK, width), block_mask.T,
        front_rest.reshape(win_blocks, BLK, front_cols), row_maps, col_maps,
    )])


def solution(mesh):
    sizes = mesh.shape["leaf"], mesh.shape["row"], mesh.shape["col"]
    return jax.shard_map(
        functools.partial(body, sizes),
        mesh=mesh,
        in_specs=(
            P(("leaf", "row"), "col"),
            P(("leaf", "row"), "col"),
            P(("leaf", "row"), "col"),
            P(("leaf", "row"), None),
            P(("leaf", "col"), None),
        ),
        out_specs=P(("leaf", "row"), "col"),
        check_vma=False,
    )
```

```python
import functools

import jax
import jax.numpy as jnp
from jax import lax
from jax.experimental import pallas as pl
from jax.experimental.pallas import tpu as pltpu
from jax.sharding import PartitionSpec as P

BLK = 128
PC = 6144
F32 = jnp.float32
BF16 = jnp.bfloat16

LEFT, RIGHT, PAIR, CROSS, DIAG = range(5)
GROUPS = ((0, 1), (6, 7), (2, 4), (3,), (5,))
STORE = tuple(slot for group in GROUPS for slot in group)
INNER = (
    "S5", "S1", "M", "S3", "A1", "S0", "A2", "S6", "x01", "S7", "S2", "x21",
    "x31", "x02", "x11", "G0", "x22", "L", "x12", "x32", "w21", "G1", "w22", "S4",
    "w32o", "w31", "G4", "G2", "w32n", "G3",
)
OUTER = (
    "x21", "S3", "S1", "S7", "A2", "x31", "x32", "x22", "S0", "A1", "A3", "S2",
    "S5", "M", "S4", "S6", "x03", "L", "x23", "x01", "G0", "x33", "x02", "w22o",
    "x11", "w21o", "G1", "w23o", "G2", "w21n", "x12", "x13", "w23n", "w32o", "w33o", "w32n",
    "w31o", "G4", "G3", "w31n", "w33n", "w22n",
)


def split(value):
    high = value.astype(BF16)
    return high, (value - high.astype(F32)).astype(BF16)


def update_kernel(
    n_leaf, n_row, n_col,
    panel_hbm, mask_hbm, front_hbm, rows_hbm, cols_hbm,
    out_ref,
    big, panel, panel_low, front, a_cat, b_cat, snd, got, mine,
    rows_own, rows_col, rows_other, cols_own, cols_other,
    mask_s, rows_own_s, rows_col_s, rows_other_s, cols_own_s, cols_other_s,
    send, recv, sib_send, sib_recv, map_send, map_recv, loc,
):
    leaf, r, c = lax.axis_index("leaf"), lax.axis_index("row"), lax.axis_index("col")
    x, k = r // 2, r % 2
    sib = lax.rem(leaf + n_leaf // 2, n_leaf)
    upper = leaf // (n_leaf // 2) % 2
    width = panel.shape[2]
    blocks, win_blocks = front.shape[:2]
    half = win_blocks // 2
    keep = half * BLK
    lanes = width // BLK
    parents = out_ref.shape[1] // BLK
    span = 3 * width

    pair_row, x_row, diag_row = x * 2 + 1 - k, (1 - x) * 2 + k, (1 - x) * 2 + 1 - k
    is_o, is_q, is_x, is_d = r == c, pair_row == c, x_row == c, diag_row == c

    def to(row=None, column=None, other_leaf=None):
        return {
            "leaf": leaf if other_leaf is None else other_leaf,
            "row": r if row is None else row,
            "col": c if column is None else column,
        }

    def remote(src, dst, ssem, rsem, where):
        return pltpu.make_async_remote_copy(
            src_ref=src, dst_ref=dst, send_sem=ssem, recv_sem=rsem,
            device_id=where, device_id_type=pl.DeviceIdType.MESH,
        )

    def push(way, src, j, dst):
        where = {
            LEFT: lambda: to(column=c - 1), RIGHT: lambda: to(column=c + 1),
            PAIR: lambda: to(row=pair_row), CROSS: lambda: to(row=x_row), DIAG: lambda: to(row=diag_row),
        }[way]()
        return remote(big.at[src, j], big.at[dst, j], send.at[way, src, j], recv.at[dst, j], where)

    sent, gates = [], []

    def when(cond, run):
        @pl.when(cond())
        def _():
            gates.append(cond)
            run()
            gates.pop()

    def go(way, copy):
        sent.append((way, copy, tuple(gates)))
        push(way, *copy()).start()

    def settle(copies, depth):
        for way, copy, conds in copies:
            def finish():
                push(way, *copy()).wait_send()
            if conds[depth:]:
                pl.when(both(*[cond() for cond in conds[depth:]]))(finish)
            else:
                finish()

    def arrive(slot, j):
        push(PAIR, slot, j, slot).wait_recv()

    def both(*conds):
        total = conds[0]
        for cond in conds[1:]:
            total = jnp.logical_and(total, cond)
        return total

    def fetch(src, dst, n):
        return pltpu.make_async_copy(src, dst, loc.at[n])

    get_rows = fetch(rows_hbm, rows_own, 0)
    get_rows_s = fetch(rows_hbm, rows_own_s, 5 + blocks)
    get_mask = fetch(mask_hbm, mask_s, 1)
    get_win = fetch(panel_hbm.at[pl.ds(0, win_blocks)], panel, 2)
    rest = pl.ds(win_blocks, blocks - win_blocks)
    get_low = fetch(panel_hbm.at[rest], panel_low, 3)
    get_cols = fetch(cols_hbm, cols_own, 4)
    get_front = [
        fetch(front_hbm.at[:, :, pl.ds(m * BLK, BLK)], front.at[m], 5 + m) for m in range(blocks)
    ]
    get_rows_s.start()
    get_mask.start()
    get_win.start()
    get_low.start()
    get_rows.start()
    get_cols.start()
    for copy in get_front:
        copy.start()

    barrier = pltpu.get_barrier_semaphore()

    def greet(where):
        pl.semaphore_signal(barrier, inc=1, device_id=where, device_id_type=pl.DeviceIdType.MESH)

    has_left, has_right = c >= 1, c + 1 < n_col

    @pl.when(has_left)
    def _():
        greet(to(column=c - 1))

    @pl.when(has_right)
    def _():
        greet(to(column=c + 1))

    greet(to(row=x_row))
    greet(to(row=diag_row))
    greet(to(other_leaf=sib))
    greet(to(row=pair_row))

    first_kept, first_sent = upper * half, (1 - upper) * half
    order_own = [first_sent + i for i in range(half)] + [first_kept + i for i in range(half)]
    order_other = [first_kept + i for i in range(half)] + [first_sent + i for i in range(half)]

    def place(rows_s, parent):
        at = jnp.int32(0)
        for m in range(1, win_blocks):
            at = jnp.where(rows_s[0, m] == parent, jnp.int32(m), at)
        return at

    def pick(values, at):
        total = jnp.int32(0)
        for m, value in enumerate(values):
            total = total + jnp.where(at == m, value, jnp.int32(0))
        return total

    get_mask.wait()
    get_rows_s.wait()
    natural = [place(rows_own_s, parent) for parent in order_own]

    def window_base(column):
        return jnp.where(r == column, 0, blocks)

    win_at = window_base(c)
    low_at = jnp.where(is_o, win_blocks, 2 * blocks)

    get_win.wait()
    for b in range(win_blocks):
        block = panel[natural[b]]
        for h in range(lanes):
            cut = slice(h * BLK, (h + 1) * BLK)
            flag = pick([mask_s[h, m] for m in range(win_blocks)], natural[b]).astype(F32)
            big[win_at + b, c, :, cut] = block[:, cut] * flag
    get_low.wait()
    for b in range(win_blocks):
        at = win_blocks + b
        for h in range(lanes):
            cut = slice(h * BLK, (h + 1) * BLK)
            big[low_at + b, c, :, cut] = panel_low[b, :, cut] * mask_s[h, at].astype(F32)

    pl.semaphore_wait(barrier, 4 + has_left.astype(jnp.int32) + has_right.astype(jnp.int32))

    transit = blocks + win_blocks

    def goal(s):
        return pair_row if s < 2 else (1 - x) * 2 + (s - 2)

    def low_slot(s, column):
        block = s if s < 2 else 2 + k
        return jnp.where(goal(s) == column, win_blocks + block, transit + s)

    def has(side):
        return has_right if side else has_left

    def next_of(side):
        return c + 1 if side else c - 1

    def from_at(side, d):
        return c - d if side else c + d

    def there(side, d):
        return from_at(side, d) >= 0 if side else from_at(side, d) < n_col

    def window_on(b, d, side):
        when(lambda: has(side), lambda: go(
            RIGHT if side else LEFT,
            lambda: (win_at + b, from_at(side, d), window_base(next_of(side)) + b),
        ))

    def hand_out(slot, j):
        for way in (CROSS, PAIR):
            go(way, lambda: (slot(), j(), slot()))

    def take_window(b, d):
        for side in (0, 1):
            def run(side=side):
                arrive(win_at + b, from_at(side, d))
                window_on(b, d, side)
                when(lambda: is_o, lambda: hand_out(lambda: b, lambda: from_at(side, d)))
            when(lambda side=side: there(side, d), run)

    def ahead(s, side):
        return goal(s) > c if side else goal(s) < c

    def low_on(s, d, side):
        go(RIGHT if side else LEFT, lambda: (low_slot(s, c), from_at(side, d), low_slot(s, next_of(side))))

    def take_low(s, d):
        for side in (0, 1):
            def wanted(side=side):
                return both(there(side, d), jnp.logical_or(ahead(s, side), goal(s) == c))

            def run(side=side):
                arrive(low_slot(s, c), from_at(side, d))
                when(lambda: ahead(s, side), lambda: low_on(s, d, side))
                when(lambda: goal(s) == c, lambda: hand_out(lambda: low_slot(s, c), lambda: from_at(side, d)))
            when(wanted, run)

    def own_low(side):
        for s in LOW:
            def run(s=s):
                arrive(transit + s, c)
                low_on(s, 0, side)
            when(lambda s=s: ahead(s, side), run)

    LOW = (2, 3, 0, 1)

    def not_o():
        return jnp.logical_not(is_o)

    def owner():
        return is_o

    def inner():
        return both(has_left, has_right)

    def outer():
        return jnp.logical_not(inner())

    def near():
        return jnp.logical_or(is_o, is_q)

    def far():
        return jnp.logical_not(near())

    def scatter():
        go(CROSS, lambda: (low_at + 2 + k, c, transit + 2 + k))
        go(DIAG, lambda: (low_at + 3 - k, c, transit + 2 + k))
        for s in range(2):
            go(PAIR, lambda s=s: (low_at + s, c, transit + s))

    def spread(slots):
        for slot in slots:
            hand_out(lambda slot=slot: slot, lambda: c)

    def at_source(side):
        return c == 0 if side else c == n_col - 1

    def own_late(side):
        for b in range(half, win_blocks):
            window_on(b, 0, side)

    def map_copy(src, dst, n, where, arrived=None):
        return remote(src, dst, map_send.at[n], map_recv.at[n if arrived is None else arrived], where)

    get_rows.wait()
    get_cols.wait()
    to_sib_cols = map_copy(cols_own, cols_other, 0, to(other_leaf=sib))
    to_sib_cols.start()
    rows_cross = map_copy(rows_own, rows_col, 1, to(row=x_row))
    rows_pair = map_copy(rows_own, rows_col, 2, to(row=pair_row), 1)
    rows_pass = map_copy(rows_col, rows_col, 2, to(row=pair_row), 1)
    rows_stay = fetch(rows_own, rows_col, 0)
    to_sib_rows = map_copy(rows_col, rows_other, 3, to(other_leaf=sib))

    def rows_from_owner():
        rows_cross.start()
        rows_pair.start()
        rows_stay.start()

    when(owner, rows_from_owner)

    def by_cross(slot, j):
        if slot < win_blocks:
            other = is_x
        elif slot < win_blocks + 2:
            other = is_d
        else:
            other = both(k == slot - win_blocks - 2, jnp.logical_or(is_o, is_q))
        return jnp.where(c == j, is_x, other)

    def by_pair(slot, j):
        if slot < win_blocks:
            other = jnp.logical_or(is_q, is_d)
        elif slot < win_blocks + 2:
            other = jnp.logical_or(is_o, is_x)
        else:
            other = k != slot - win_blocks - 2
        return jnp.where(c == j, jnp.logical_or(is_q, is_d), other)

    def collect(slots):
        for slot in slots:
            for j in range(n_col):
                def run(slot=slot, j=j):
                    arrive(slot, j)
                    go(PAIR, lambda: (slot, j, slot))
                when(lambda slot=slot, j=j: by_cross(slot, j), run)
        for slot in slots:
            for j in range(n_col):
                when(lambda slot=slot, j=j: by_pair(slot, j), lambda: arrive(slot, j))

    def lay_rows(b):
        rows = slice(b * BLK, (b + 1) * BLK)
        for j in range(n_col):
            high, low = split(big[win_at + b, j])
            at = j * span
            a_cat[rows, at:at + width] = high
            a_cat[rows, at + width:at + 2 * width] = high
            a_cat[rows, at + 2 * width:at + span] = low

    def lay_columns(slot):
        rows = slice(STORE.index(slot) * BLK, (STORE.index(slot) + 1) * BLK)
        for j in range(n_col):
            high, low = split(big[slot, j])
            at = j * span
            b_cat[rows, at:at + width] = high
            b_cat[rows, at + width:at + 2 * width] = low
            b_cat[rows, at + 2 * width:at + span] = high

    def multiply(slots, part):
        first = STORE.index(slots[0])
        product = lax.dot_general(
            a_cat[part * keep:(part + 1) * keep, :], b_cat[first * BLK:(first + len(slots)) * BLK, :],
            (((1,), (1,)), ((), ())), preferred_element_type=F32,
        )
        into = mine if part else snd
        for i, slot in enumerate(slots):
            column = place(rows_col_s, order_own[slot]) if slot < win_blocks else slot
            for b in range(half):
                into[slot, b * BLK:(b + 1) * BLK, :] = (
                    front[column, natural[part * half + b]] - product[b * BLK:(b + 1) * BLK, i * BLK:(i + 1) * BLK]
                )

    def sibling(slot):
        return remote(snd.at[slot], got.at[slot], sib_send.at[slot], sib_recv.at[slot], to(other_leaf=sib))

    def group_out(group):
        slots = GROUPS[group]
        collect(slots)
        if group == 0:
            for b in range(half):
                lay_rows(b)
            for copy in get_front:
                copy.wait()
        for slot in slots:
            lay_columns(slot)
        multiply(slots, 0)
        for slot in slots:
            sibling(slot).start()

    def maps_in():
        when(owner, lambda: rows_stay.wait())
        when(not_o, lambda: rows_cross.wait_recv())
        when(lambda: is_x, lambda: rows_pass.start())
        to_sib_rows.start()
        to_col_s = fetch(rows_col, rows_col_s, 0)
        to_col_s.start()
        to_col_s.wait()

    def windows(d):
        for b in range(half):
            take_window(b, d)
        for side in (0, 1):
            last = 0 if side else n_col - 1
            when(lambda side=side, last=last: from_at(side, d) == last, functools.partial(own_low, side))

    def own_rest():
        for side in (0, 1):
            when(lambda side=side: jnp.logical_not(at_source(side)), functools.partial(own_late, side))

    def step(token):
        kind, rest = token[0], token[1:]
        if kind == "A":
            windows(int(rest))
        elif kind == "S":
            when(owner, functools.partial(spread, (int(rest),)))
        elif kind == "M":
            maps_in()
        elif kind == "L":
            own_rest()
        elif kind == "G":
            group_out(int(rest))
        elif kind == "x":
            take_low(int(rest[0]), int(rest[1]))
        else:
            run = functools.partial(take_window, int(rest[0]), int(rest[1]))
            if rest[2:]:
                when(owner if rest[2:] == "o" else not_o, run)
            else:
                run()

    def follow(tokens):
        for token in tokens:
            step(token)

    for b in range(half):
        for side in (0, 1):
            window_on(b, 0, side)
    when(not_o, scatter)
    for side in (0, 1):
        def source(side=side):
            own_low(side)
            own_late(side)
        when(lambda side=side: at_source(side), source)

    first = len(sent)
    parts = []
    for mine_too, tokens in ((inner, INNER), (outer, OUTER)):
        before = len(sent)
        when(mine_too, functools.partial(follow, tokens))
        parts.append((mine_too, sent[before:]))
    for b in range(half, win_blocks):
        lay_rows(b)
    for slots in GROUPS:
        multiply(slots, 1)
    for mine_too, copies in parts:
        when(mine_too, functools.partial(settle, copies, 1))
    settle(sent[:first], 0)

    to_sib_cols.wait_recv()
    to_sib_rows.wait_recv()
    to_own = fetch(cols_own, cols_own_s, 1)
    to_other = fetch(cols_other, cols_other_s, 2)
    to_rows = fetch(rows_other, rows_other_s, 3)
    to_own.start()
    to_other.start()
    to_rows.start()
    to_own.wait()
    to_other.wait()
    to_rows.wait()
    natural_col = [place(rows_col_s, parent) for parent in order_own]
    natural_other = [place(rows_other_s, parent) for parent in order_other]

    def spots(cols_s, naturals):
        values = [cols_s[0, m] for m in range(blocks)]
        return [pick(values[:win_blocks], naturals[o]) if o < win_blocks else values[o] for o in range(blocks)]

    spot_own, spot_other = spots(cols_own_s, natural_col), spots(cols_other_s, natural_other)

    def source_of(spot, t):
        at, found = jnp.int32(0), jnp.int32(0)
        for o in range(blocks):
            hit = spot[o] == t
            at, found = jnp.where(hit, jnp.int32(o), at), jnp.where(hit, jnp.int32(1), found)
        return at, found.astype(F32)

    sources = [(source_of(spot_own, t), source_of(spot_other, t)) for t in range(parents)]
    for o in range(blocks):
        sibling(o).wait_recv()
    for t, ((at, found), (at_got, found_got)) in enumerate(sources):
        out_ref[:, t * BLK:(t + 1) * BLK] = mine[at] * found + got[at_got] * found_got

    for o in range(blocks):
        sibling(o).wait_send()
    to_sib_cols.wait_send()
    to_sib_rows.wait_send()
    when(owner, lambda: rows_cross.wait_send())
    when(owner, lambda: rows_pair.wait_send())
    when(lambda: is_x, lambda: rows_pass.wait_send())


def body(sizes, panel, block_mask, front_rest, row_maps, col_maps):
    n_leaf, n_row, n_col = sizes
    local_rows, width = panel.shape
    win_rows, front_cols = front_rest.shape
    keep = win_rows // 2
    blocks = front_cols // BLK
    win_blocks = win_rows // BLK
    parent_cols = PC // n_col
    any_space = pl.BlockSpec(memory_space=pl.ANY)
    dma = pltpu.SemaphoreType.DMA
    slots = 2 * blocks + win_blocks
    rows_type, cols_type = row_maps.dtype, col_maps.dtype
    return pl.pallas_call(
        functools.partial(update_kernel, n_leaf, n_row, n_col),
        out_shape=jax.ShapeDtypeStruct((keep, parent_cols), F32),
        in_specs=[any_space] * 5,
        out_specs=pl.BlockSpec(memory_space=pltpu.VMEM),
        scratch_shapes=[
            pltpu.VMEM((slots, n_col, BLK, width), F32),
            pltpu.VMEM((win_blocks, BLK, width), F32),
            pltpu.VMEM((blocks - win_blocks, BLK, width), F32),
            pltpu.VMEM((blocks, win_blocks, BLK, BLK), F32),
            pltpu.VMEM((win_rows, 3 * n_col * width), BF16),
            pltpu.VMEM((blocks * BLK, 3 * n_col * width), BF16),
            pltpu.VMEM((blocks, keep, BLK), F32),
            pltpu.VMEM((blocks, keep, BLK), F32),
            pltpu.VMEM((blocks, keep, BLK), F32),
            pltpu.VMEM(row_maps.shape, rows_type), pltpu.VMEM(row_maps.shape, rows_type),
            pltpu.VMEM(row_maps.shape, rows_type),
            pltpu.VMEM(col_maps.shape, cols_type), pltpu.VMEM(col_maps.shape, cols_type),
            pltpu.SMEM(block_mask.shape[::-1], block_mask.dtype),
            pltpu.SMEM(row_maps.shape, rows_type), pltpu.SMEM(row_maps.shape, rows_type),
            pltpu.SMEM(row_maps.shape, rows_type),
            pltpu.SMEM(col_maps.shape, cols_type), pltpu.SMEM(col_maps.shape, cols_type),
            dma((5, slots, n_col)), dma((slots, n_col)),
            dma((blocks,)), dma((blocks,)), dma((4,)), dma((4,)), dma((6 + blocks,)),
        ],
        compiler_params=pltpu.CompilerParams(
            collective_id=0, has_side_effects=True, vmem_limit_bytes=40 * 1024 * 1024
        ),
        name="update",
    )(*[pltpu.with_memory_space_constraint(value, pltpu.HBM) for value in (
        panel.reshape(local_rows // BLK, BLK, width), block_mask.T,
        front_rest.reshape(win_blocks, BLK, front_cols), row_maps, col_maps,
    )])


def solution(mesh):
    sizes = mesh.shape["leaf"], mesh.shape["row"], mesh.shape["col"]
    return jax.shard_map(
        functools.partial(body, sizes),
        mesh=mesh,
        in_specs=(
            P(("leaf", "row"), "col"),
            P(("leaf", "row"), "col"),
            P(("leaf", "row"), "col"),
            P(("leaf", "row"), None),
            P(("leaf", "col"), None),
        ),
        out_specs=P(("leaf", "row"), "col"),
        check_vma=False,
    )
```
